32 devices in a mesh: seq: 8 (over z, x), head: 4 (over y, core).
Axes of the slice: x: 2, y: 2, z: 4, core: 2. Of those that a mesh axis runs over, the one named last changes fastest.
Arguments:
- queries: bfloat16 [8192, 32, 128], P('seq', 'head'), may hold values from -13 to 13, as said below
- keys: bfloat16 [8192, 8, 128], P('seq', 'head'), may hold values from -13 to 13, as said below
- values: bfloat16 [8192, 8, 128], P('seq', 'head'), may hold values from -18 to 18
- vertical_blocks: int32 [8, 24], P('head'), may hold values from 0 to 63, as said below
- band_offsets: int32 [8, 4], P('head'), may hold values from 0 to 896, as said below
- out_weight: bfloat16 [4096, 4096], P('head'), may hold values from -0.125 to 0.125
Outputs:
- mixed: bfloat16 [8192, 4096], P('seq', 'head')
The draws below stay inside these ranges and needn't reach their ends.
Inputs may be any that keep to these rules, and one draw needn't show every extreme that they name: queries in both draws lie within this range. keys in both draws lie within this range. `vertical_blocks`: each row lists 24 different key blocks in increasing order; blocks 0 to 3 and the last block are in every row; the 1024 tokens of one index of seq hold at most 4 of a row's blocks. `band_offsets`: each row holds 4 different multiples of 128 in increasing order, among them 0 and 896.
All inputs are finite; a program needn't handle non-finite values.
Results may differ from the reference program's by a relative error of at most 0.02.
Values may be sent and summed in bfloat16 or wider, within the bound.
A program may use at most 128 MiB of HBM per device.

```python
import jax
import jax.numpy as jnp
from jax import lax

D = 4096
QH = 32
KVH = 8
HD = 128
TOK_DEV = 1024
BLK = 128
NV = 24
NS = 4
VCAP = 4
QPK = 4
TOKENS = 8192
N_HEAD = 4


def draw_queries(key, part):
    inner_key = jax.random.fold_in(key, 1)
    drawn = 1.5 * jax.random.truncated_normal(inner_key, -6.0, 6.0, (TOKENS, QH, HD), jnp.float32)
    return drawn.astype(jnp.bfloat16)


def draw_keys(key, part):
    inner_key = jax.random.fold_in(key, 2)
    drawn = 1.5 * jax.random.truncated_normal(inner_key, -6.0, 6.0, (TOKENS, KVH, HD), jnp.float32)
    return drawn.astype(jnp.bfloat16)


def vertical_row(key):
    per_shard = TOK_DEV // BLK
    shard_count = TOKENS // TOK_DEV
    split_keys = jax.random.split(key, shard_count + 1)

    def front(shard_key):
        return jax.random.permutation(shard_key, per_shard)[:VCAP]
    middle_picks = jax.vmap(front)(split_keys[:shard_count - 2])
    middle = (middle_picks + (jnp.arange(1, shard_count - 1, dtype=jnp.int32) * per_shard)[:, None]).reshape(-1)
    tail = jax.random.permutation(split_keys[shard_count - 2], per_shard - 1)[:VCAP - 1] + (shard_count - 1) * per_shard
    final_block = jnp.array([shard_count * per_shard - 1], jnp.int32)
    candidates = jnp.concatenate([middle.astype(jnp.int32), tail.astype(jnp.int32)])
    chosen = jax.random.permutation(split_keys[shard_count - 1], candidates)[:NV - VCAP - 1]
    return jnp.sort(jnp.concatenate([jnp.arange(VCAP, dtype=jnp.int32), final_block, chosen]))


def draw_vertical_blocks(key, part):
    return jax.vmap(vertical_row)(jax.random.split(key, KVH))


def band_row(key):
    per_shard = TOK_DEV // BLK
    inner_pick = (jax.random.permutation(key, per_shard - 2) + 1)[:NS - 2].astype(jnp.int32)
    ends = jnp.array([0, per_shard - 1], jnp.int32)
    return jnp.sort(jnp.concatenate([ends, inner_pick])) * BLK


def draw_band_offsets(key, part):
    return jax.vmap(band_row)(jax.random.split(jax.random.fold_in(key, 5), KVH))


def spiked(result, stream_key, source, target, parts, factor):
    def block_of(axis_at):
        return (jnp.arange(result.shape[axis_at]) // (result.shape[axis_at] // parts)).reshape((-1,) + (1,) * (result.ndim - 1 - axis_at))

    near = jax.random.permutation(stream_key, parts)[block_of(target)]
    far = (block_of(target) + parts // 2) % parts
    return jnp.where((block_of(source) == near) | (block_of(source) == far), factor * result, result)


def level_of(stream_key, dims, cuts, smallest, high):
    def one(dim, shards_of):
        steps = jax.random.uniform(jax.random.fold_in(jax.random.fold_in(stream_key, 6), dim), (shards_of,), jnp.float32, smallest / len(cuts), high / len(cuts))
        return jnp.repeat(jnp.exp(steps), dims[dim] // shards_of).reshape((-1,) + (1,) * (len(dims) - dim - 1))

    loudness = one(*cuts[0])
    for cut in cuts[1:]:
        loudness = loudness * one(*cut)
    return loudness


def normal_values(key, dims, scale, reach, cuts=(), kind=jnp.bfloat16):
    level = level_of(key, dims, cuts, -0.22, 0.18) if cuts else 1.0
    values = jax.random.normal(key, dims, jnp.float32) * scale * level
    return jnp.minimum(jnp.maximum(values, -reach), reach).astype(kind)


def noise_with(stream_key, extent, deviation, most, cuts, heavy, kind=jnp.bfloat16):
    entries = deviation * jax.random.normal(stream_key, extent, jnp.float32)
    if cuts:
        entries = entries * level_of(stream_key, extent, cuts, -0.22, 0.18)
    return jnp.clip(spiked(entries, jax.random.fold_in(stream_key, 3), *heavy), -most, most).astype(kind)


def setup_inputs(seed: int = 0) -> dict:
    splits = jax.random.split(jax.random.key(seed), 7)
    queries = draw_queries(jax.random.fold_in(splits[6], 71), 0)
    keys = draw_keys(jax.random.fold_in(splits[6], 71), 0)
    values = normal_values(splits[2], (TOKENS, KVH, HD), 3.0, 18.0, ((0, 8), (1, 4)))
    vertical_blocks = draw_vertical_blocks(jax.random.fold_in(splits[6], 71), 0)
    band_offsets = draw_band_offsets(jax.random.fold_in(splits[6], 71), 0)
    out_weight = noise_with(splits[5], (QH * HD, D), (QH * HD) ** -0.5, 0.125, ((0, 4),), (0, 1, 4, 2.0))
    return {"queries": queries, "keys": keys, "values": values, "vertical_blocks": vertical_blocks, "band_offsets": band_offsets, "out_weight": out_weight}


masked_score = -1e30


def head_block(query_block, head_keys, head_values, vert_list, band_list, anchor):
    span_rows = query_block.shape[0]
    width = span_rows + TOK_DEV
    block_count = head_keys.shape[0] // BLK
    vert_keys = head_keys.reshape(block_count, BLK, HD)[vert_list].reshape(NV * BLK, HD)
    vert_values = head_values.reshape(block_count, BLK, HD)[vert_list].reshape(NV * BLK, HD)
    vert_pos = (vert_list[:, None] * BLK + jnp.arange(BLK, dtype=jnp.int32)[None, :]).reshape(NV * BLK)
    padding = jnp.zeros((TOK_DEV, HD), head_keys.dtype)
    window_keys = lax.dynamic_slice_in_dim(jnp.concatenate([padding, head_keys], 0), anchor, width, 0)
    window_values = lax.dynamic_slice_in_dim(jnp.concatenate([padding, head_values], 0), anchor, width, 0)
    window_pos = anchor - TOK_DEV + jnp.arange(width, dtype=jnp.int32)
    query_pos = anchor + jnp.arange(span_rows, dtype=jnp.int32)
    listed = jnp.any((window_pos[:, None] // BLK) == vert_list[None, :], axis=1)
    distance = query_pos[:, None] - window_pos[None, :]
    on_band = jnp.any(((distance // BLK) * BLK)[:, :, None] == band_list[None, None, :], axis=2)
    band_mask = on_band & (distance >= 0) & (window_pos >= 0)[None, :] & jnp.logical_not(listed)[None, :]
    vert_mask = vert_pos[None, :] <= query_pos[:, None]
    allowed = jnp.concatenate([vert_mask, band_mask], axis=1)
    key_rows = jnp.concatenate([vert_keys, window_keys], axis=0)
    value_rows = jnp.concatenate([vert_values, window_values], axis=0)
    scores = jnp.einsum('qhd,kd->hqk', query_block.astype(jnp.float32), key_rows.astype(jnp.float32)) * (HD ** -0.5)
    scores = jnp.where(allowed[None], scores, masked_score)
    row_top = jnp.max(scores, axis=2, keepdims=True)
    weights = jnp.where(allowed[None], jnp.exp(scores - row_top), 0.0)
    weight_sum = jnp.sum(weights, axis=2)
    probs = lax.optimization_barrier(weights.astype(jnp.bfloat16))
    attended = jnp.einsum('hqk,kd->hqd', probs.astype(jnp.float32), value_rows.astype(jnp.float32))
    attended = attended / weight_sum[:, :, None]
    return attended.astype(jnp.bfloat16)


def reference(queries, keys, values, vertical_blocks, band_offsets, out_weight):
    block_rows = TOKENS // TOK_DEV

    def per_head(head):
        head_keys = lax.dynamic_index_in_dim(keys, head, 1, keepdims=False)
        head_values = lax.dynamic_index_in_dim(values, head, 1, keepdims=False)
        head_queries = lax.dynamic_slice_in_dim(queries, head * QPK, QPK, 1)
        vert_list = vertical_blocks[head]
        band_list = band_offsets[head]

        def per_block(index):
            anchor = index * TOK_DEV
            query_block = lax.dynamic_slice_in_dim(head_queries, anchor, TOK_DEV, 0)
            return head_block(query_block, head_keys, head_values, vert_list, band_list, anchor)

        return lax.map(per_block, jnp.arange(block_rows, dtype=jnp.int32))

    results = lax.map(per_head, jnp.arange(KVH, dtype=jnp.int32))
    attended = results.transpose(1, 3, 0, 2, 4).reshape(TOKENS, QH * HD)
    group_width = QH * HD // N_HEAD
    grouped = attended.reshape(TOKENS, N_HEAD, group_width)
    weight_groups = out_weight.reshape(N_HEAD, group_width, D)

    def add_group(group, running):
        partial_term = jnp.dot(grouped[:, group], weight_groups[group], preferred_element_type=jnp.float32)
        partial_term = lax.optimization_barrier(partial_term.astype(jnp.bfloat16))
        return running + partial_term.astype(jnp.float32)

    mixed = lax.fori_loop(0, N_HEAD, add_group, jnp.zeros((TOKENS, D), jnp.float32))
    return mixed.astype(jnp.bfloat16)
```

```python
import functools

import jax
import jax.numpy as jnp
from jax import lax
from jax.experimental import pallas as pl
from jax.experimental.pallas import tpu as pltpu
from jax.sharding import PartitionSpec as P

BLK = 128
MASKED = -1e30
MESH = pl.DeviceIdType.MESH
LOG2E = 1.4426950408889634


def attend_kernel(
    n_head,
    slot_cap,
    proj_rows,
    q_ref,
    kext_ref,
    vext_ref,
    kslot_ref,
    vslot_ref,
    wbias_ref,
    sbias_ref,
    w_hbm,
    out_ref,
    w_ref,
    att_ref,
    own_ref,
    msend_ref,
    mrecv_ref,
    ysend_ref,
    yrecv_ref,
    w_sem,
    msend_sem,
    mrecv_sem,
    ysend_sem,
    yrecv_sem,
):
    seq = lax.axis_index("seq")
    head = lax.axis_index("head")
    core = lax.rem(head, 2)
    y_at = head // 2
    n_y = n_head // 2
    mate = y_at * 2 + 1 - core
    kv_local, blocks, rows, head_dim = q_ref.shape
    group = rows // BLK
    window = (blocks + 1) * BLK
    step_keys = slot_cap * BLK
    width = w_ref.shape[1] // n_head
    chunks = blocks * BLK // proj_rows
    per_chunk = proj_rows // BLK
    scale = head_dim ** (-0.5) * LOG2E

    def y_peer(k):
        return lax.rem(y_at + k, n_y)

    w_copy = pltpu.make_async_copy(w_hbm, w_ref, w_sem)
    w_copy.start()
    barrier = pltpu.get_barrier_semaphore()
    pl.semaphore_signal(barrier, inc=1, device_id=(seq, mate), device_id_type=MESH)
    for k in range(1, n_y):
        pl.semaphore_signal(
            barrier, inc=1, device_id=(seq, y_peer(k) * 2 + core), device_id_type=MESH
        )
    pl.semaphore_wait(barrier, n_y)

    row_at = lax.broadcasted_iota(jnp.int32, (BLK, window), 0)
    col_at = lax.broadcasted_iota(jnp.int32, (BLK, window), 1) & (BLK - 1)
    lower = col_at <= row_at

    def attend(h, b, local):
        start = pl.multiple_of(b * BLK, BLK)
        q = q_ref[h, b]
        nt = (((1,), (1,)), ((), ()))
        s = lax.dot_general(
            q, kext_ref[h, pl.ds(start, window), :], nt, preferred_element_type=jnp.float32
        )
        bias = jnp.where(
            lower, wbias_ref[h, 0, pl.ds(b, 1), :], wbias_ref[h, 1, pl.ds(b, 1), :]
        )
        s = (s.reshape(group, BLK, window) + bias[None]).reshape(rows, window)
        top = jnp.max(s, axis=1, keepdims=True)
        p = jnp.exp2((s - top) * scale).astype(jnp.bfloat16)
        acc = jnp.dot(
            p, vext_ref[h, pl.ds(start, window), :], preferred_element_type=jnp.float32
        )

        def absorb(j, running):
            top, acc = running
            at = pl.multiple_of(j * step_keys, step_keys)
            s = lax.dot_general(
                q, kslot_ref[h, pl.ds(at, step_keys), :], nt, preferred_element_type=jnp.float32
            )
            s = s + sbias_ref[h, pl.ds(b, 1), pl.ds(at, step_keys)]
            new_top = jnp.maximum(top, jnp.max(s, axis=1, keepdims=True))
            p = jnp.exp2((s - new_top) * scale).astype(jnp.bfloat16)
            acc = acc * jnp.exp2((top - new_top) * scale) + jnp.dot(
                p, vslot_ref[h, pl.ds(at, step_keys), :], preferred_element_type=jnp.float32
            )
            return new_top, acc

        top, acc = lax.fori_loop(0, seq, absorb, (top, acc))
        done = (acc[:, :head_dim] / acc[:, head_dim:]).astype(jnp.bfloat16)
        for g in range(group):
            at = pl.multiple_of((h * group + g) * head_dim, head_dim)
            att_ref[pl.ds(local * BLK, BLK), pl.ds(at, head_dim)] = done[g * BLK : (g + 1) * BLK]

    def mate_copy(t):
        return pltpu.make_async_remote_copy(
            src_ref=msend_ref.at[t],
            dst_ref=mrecv_ref.at[t],
            send_sem=msend_sem.at[t],
            recv_sem=mrecv_sem.at[t],
            device_id=(seq, mate),
            device_id_type=MESH,
        )

    def y_copy(t, k):
        return pltpu.make_async_remote_copy(
            src_ref=ysend_ref.at[t, k - 1],
            dst_ref=yrecv_ref.at[t, n_y - k - 1],
            send_sem=ysend_sem.at[t, k - 1],
            recv_sem=yrecv_sem.at[t, n_y - k - 1],
            device_id=(seq, y_peer(k) * 2 + core),
            device_id_type=MESH,
        )

    def pass_on(t):
        mate_copy(t).wait_recv()
        for k in range(1, n_y):
            ysend_ref[t, k - 1] = (
                own_ref[t, k].astype(jnp.float32) + mrecv_ref[t, k].astype(jnp.float32)
            ).astype(jnp.bfloat16)
            y_copy(t, k).start()

    def finish(t):
        total = own_ref[t, 0].astype(jnp.float32) + mrecv_ref[t, 0].astype(jnp.float32)
        for k in range(1, n_y):
            y_copy(t, k).wait_recv()
        for k in range(1, n_y):
            total = total + yrecv_ref[t, n_y - k - 1].astype(jnp.float32)
        out_ref[pl.ds(pl.multiple_of(t * proj_rows, proj_rows), proj_rows), :] = total.astype(
            jnp.bfloat16
        )
        mate_copy(t).wait_send()
        for k in range(1, n_y):
            y_copy(t, k).wait_send()

    def project(t):
        for k in range(n_y - 1, -1, -1):
            for target, dest in ((1 - core, msend_ref), (core, own_ref)):
                at = pl.multiple_of((y_peer(k) * 2 + target) * width, width)
                dest[t, k] = jnp.dot(
                    att_ref[...], w_ref[:, pl.ds(at, width)], preferred_element_type=jnp.float32
                ).astype(jnp.bfloat16)

    def chunk(t, carry):
        def part(i, c):
            local = i // kv_local
            attend(lax.rem(i, kv_local), t * per_chunk + local, local)

            @pl.when((i == 0) & (t > 0))
            def _():
                pass_on(t - 1)

            return c

        lax.fori_loop(0, per_chunk * kv_local, part, 0)

        @pl.when(t == 0)
        def _():
            w_copy.wait()

        @pl.when(t > 1)
        def _():
            finish(t - 2)

        project(t)
        mate_copy(t).start()
        return carry

    lax.fori_loop(0, chunks, chunk, 0)
    pass_on(chunks - 1)
    if chunks > 1:
        finish(chunks - 2)
    finish(chunks - 1)


def on_device(n_head, queries, keys, values, vertical_blocks, band_offsets, out_weight):
    tok_rows, heads_local, head_dim = queries.shape
    kv_local = keys.shape[1]
    group = heads_local // kv_local
    blocks = tok_rows // BLK
    list_len = vertical_blocks.shape[1]
    n_seq = lax.axis_size("seq")
    slot_cap = max(2, (list_len + n_seq - 2) // (n_seq - 1))
    slots = n_seq * slot_cap
    shard = lax.axis_index("seq")
    n_y = n_head // 2
    proj_rows = 2 * BLK
    chunks = tok_rows // proj_rows
    d_model = out_weight.shape[1]
    width = d_model // n_head

    key_value = jnp.stack([jnp.swapaxes(keys, 0, 1), jnp.swapaxes(values, 0, 1)], axis=1)
    earlier = lax.ppermute(key_value, "seq", [(i, i + 1) for i in range(n_seq - 1)])
    owner = vertical_blocks // blocks
    entry = jnp.arange(list_len, dtype=jnp.int32)
    rank = jnp.sum(
        ((owner[:, :, None] == owner[:, None, :]) & (entry[None, None, :] < entry[None, :, None])).astype(
            jnp.int32
        ),
        axis=2,
    )
    where_slot = owner * slot_cap + rank
    slot_hit = where_slot[:, None, :] == jnp.arange(slots, dtype=jnp.int32)[None, :, None]
    slot_block = jnp.sum(jnp.where(slot_hit, vertical_blocks[:, None, :] + 1, 0), axis=2) - 1
    mine = lax.dynamic_slice_in_dim(slot_block, shard * slot_cap, slot_cap, 1)
    local_idx = jnp.where(mine >= 0, mine - shard * blocks, 0)
    local_blocks = key_value.reshape(kv_local, 2, blocks, BLK, head_dim)
    outgoing = jnp.stack(
        [jnp.take(local_blocks[h], local_idx[h], axis=1) for h in range(kv_local)], axis=0
    )
    gathered = lax.all_gather(outgoing, "seq", axis=2, tiled=True).reshape(
        kv_local, 2, slots * BLK, head_dim
    )
    extended = jnp.concatenate([earlier, key_value], axis=2)

    def with_ones(v):
        return jnp.concatenate([v, jnp.ones_like(v)], axis=2)

    b_at = jnp.arange(blocks, dtype=jnp.int32)
    first = (shard - 1) * blocks + b_at
    slot_ok = (slot_block >= 0)[:, None, :] & (slot_block[:, None, :] < first[None, :, None])
    slot_bias = jnp.repeat(jnp.where(slot_ok, 0.0, MASKED).astype(jnp.float32), BLK, axis=2)
    w_at = jnp.arange(blocks + 1, dtype=jnp.int32)
    blk = first[:, None] + w_at[None, :]
    dist = blocks - w_at
    listed = jnp.any(blk[None, :, :, None] == vertical_blocks[:, None, None, :], axis=3)
    back = band_offsets // BLK
    on_low = jnp.any(back[:, None, :] == dist[None, :, None], axis=2)
    on_up = jnp.any(back[:, None, :] == dist[None, :, None] - 1, axis=2)
    low = (blk >= 0)[None] & (listed | on_low[:, None, :])
    up = ((blk >= 0) & (dist >= 1)[None, :])[None] & (listed | on_up[:, None, :])
    win_bias = jnp.where(jnp.stack([low, up], axis=1), 0.0, MASKED).astype(jnp.float32)
    win_bias = jnp.repeat(win_bias, BLK, axis=3)

    q = queries.reshape(blocks, BLK, kv_local, group, head_dim)
    q = jnp.transpose(q, (2, 0, 3, 1, 4)).reshape(kv_local, blocks, group * BLK, head_dim)

    vmem = pl.BlockSpec(memory_space=pltpu.VMEM)
    piece = (proj_rows, width)
    return pl.pallas_call(
        functools.partial(attend_kernel, n_head, slot_cap, proj_rows),
        out_shape=jax.ShapeDtypeStruct((tok_rows, width), jnp.bfloat16),
        in_specs=[vmem] * 7 + [pl.BlockSpec(memory_space=pl.ANY)],
        out_specs=vmem,
        scratch_shapes=[
            pltpu.VMEM(out_weight.shape, jnp.bfloat16),
            pltpu.VMEM((proj_rows, heads_local * head_dim), jnp.bfloat16),
            pltpu.VMEM((chunks, n_y) + piece, jnp.bfloat16),
            pltpu.VMEM((chunks, n_y) + piece, jnp.bfloat16),
            pltpu.VMEM((chunks, n_y) + piece, jnp.bfloat16),
            pltpu.VMEM((chunks, n_y - 1) + piece, jnp.bfloat16),
            pltpu.VMEM((chunks, n_y - 1) + piece, jnp.bfloat16),
            pltpu.SemaphoreType.DMA,
            pltpu.SemaphoreType.DMA((chunks,)),
            pltpu.SemaphoreType.DMA((chunks,)),
            pltpu.SemaphoreType.DMA((chunks, n_y - 1)),
            pltpu.SemaphoreType.DMA((chunks, n_y - 1)),
        ],
        compiler_params=pltpu.CompilerParams(
            collective_id=0, has_side_effects=True, vmem_limit_bytes=60 << 20
        ),
    )(
        q,
        extended[:, 0],
        with_ones(extended[:, 1]),
        gathered[:, 0],
        with_ones(gathered[:, 1]),
        win_bias,
        slot_bias,
        out_weight,
    )


def solution(mesh):
    return jax.shard_map(
        functools.partial(on_device, mesh.shape["head"]),
        mesh=mesh,
        in_specs=(
            P("seq", "head", None),
            P("seq", "head", None),
            P("seq", "head", None),
            P("head", None),
            P("head", None),
            P("head", None),
        ),
        out_specs=P("seq", "head"),
        check_vma=False,
    )
```

```python
import functools

import jax
import jax.numpy as jnp
from jax import lax
from jax.experimental import pallas as pl
from jax.experimental.pallas import tpu as pltpu
from jax.sharding import PartitionSpec as P

BLK = 128
MASKED = -1e30
MESH = pl.DeviceIdType.MESH
LOG2E = 1.4426950408889634


def attend_kernel(
    n_head,
    slot_cap,
    proj_rows,
    q_ref,
    kext_ref,
    vext_ref,
    kslot_ref,
    vslot_ref,
    wbias_ref,
    sbias_ref,
    w_hbm,
    out_ref,
    w_ref,
    att_ref,
    own_ref,
    msend_ref,
    mrecv_ref,
    ysend_ref,
    yrecv_ref,
    w_sem,
    msend_sem,
    mrecv_sem,
    ysend_sem,
    yrecv_sem,
):
    seq = lax.axis_index("seq")
    head = lax.axis_index("head")
    core = lax.rem(head, 2)
    y_at = head // 2
    n_y = n_head // 2
    mate = y_at * 2 + 1 - core
    kv_local, blocks, head_dim, rows = q_ref.shape
    slots = kslot_ref.shape[1] // BLK
    group = rows // BLK
    window = (blocks + 1) * BLK
    step_keys = slot_cap * BLK
    width = w_ref.shape[1] // n_head
    chunks = blocks * BLK // proj_rows
    per_chunk = proj_rows // BLK
    scale = head_dim ** (-0.5) * LOG2E

    def y_peer(k):
        return lax.rem(y_at + k, n_y)

    w_copy = pltpu.make_async_copy(w_hbm, w_ref, w_sem)
    w_copy.start()
    barrier = pltpu.get_barrier_semaphore()
    pl.semaphore_signal(barrier, inc=1, device_id=(seq, mate), device_id_type=MESH)
    for k in range(1, n_y):
        pl.semaphore_signal(
            barrier, inc=1, device_id=(seq, y_peer(k) * 2 + core), device_id_type=MESH
        )
    pl.semaphore_wait(barrier, n_y)

    half = 2 * BLK
    key_at = lax.broadcasted_iota(jnp.int32, (BLK, half), 0)
    query_at = lax.broadcasted_iota(jnp.int32, (BLK, half), 1) & (BLK - 1)
    lower = key_at <= query_at

    def tiles(s, biases):
        return [s[i * BLK : (i + 1) * BLK] + bias for i, bias in enumerate(biases)]

    def peak(parts):
        most = parts[0]
        for part in parts[1:]:
            most = jnp.maximum(most, part)
        return jnp.max(most, axis=0, keepdims=True)

    def weigh(parts, top):
        weights = [jnp.exp2((part - top) * scale) for part in parts]
        total = weights[0]
        for weight in weights[1:]:
            total = total + weight
        probs = jnp.concatenate([weight.astype(jnp.bfloat16) for weight in weights], axis=0)
        return jnp.sum(total, axis=0, keepdims=True), probs

    def attend(h, b, local):
        start = pl.multiple_of(b * BLK, BLK)
        halves = rows // half
        at_w = (h * blocks + b) * (2 * (blocks + 1))
        at_s = (h * blocks + b) * slots
        qs = [q_ref[h, b, :, i * half : (i + 1) * half] for i in range(halves)]
        biases = [
            jnp.where(lower, wbias_ref[at_w + w], wbias_ref[at_w + blocks + 1 + w])
            for w in range(blocks + 1)
        ]
        first = []
        for q in qs:
            s = jnp.dot(
                kext_ref[h, pl.ds(start, window), :], q, preferred_element_type=jnp.float32
            )
            parts = tiles(s, biases)
            top = peak(parts)
            total, probs = weigh(parts, top)
            acc = jnp.dot(
                vext_ref[h, :, pl.ds(start, window)], probs, preferred_element_type=jnp.float32
            )
            first.append((top, total, acc))

        def absorb(j, running):
            at = pl.multiple_of(j * step_keys, step_keys)
            biases = [sbias_ref[at_s + j * slot_cap + r] for r in range(slot_cap)]
            after = []
            for q, (top, total, acc) in zip(qs, running):
                s = jnp.dot(
                    kslot_ref[h, pl.ds(at, step_keys), :], q, preferred_element_type=jnp.float32
                )
                parts = tiles(s, biases)
                new_top = jnp.maximum(top, peak(parts))
                rescale = jnp.exp2((top - new_top) * scale)
                part_sum, probs = weigh(parts, new_top)
                acc = acc * rescale + jnp.dot(
                    vslot_ref[h, :, pl.ds(at, step_keys)],
                    probs,
                    preferred_element_type=jnp.float32,
                )
                after.append((new_top, total * rescale + part_sum, acc))
            return tuple(after)

        done = lax.fori_loop(0, seq, absorb, tuple(first))
        for i, (_, total, acc) in enumerate(done):
            normed = acc / total
            for g in range(2):
                at = pl.multiple_of((h * group + 2 * i + g) * head_dim, head_dim)
                att_ref[pl.ds(local * BLK, BLK), pl.ds(at, head_dim)] = jnp.transpose(
                    normed[:, g * BLK : (g + 1) * BLK]
                ).astype(jnp.bfloat16)

    def mate_copy(t):
        return pltpu.make_async_remote_copy(
            src_ref=msend_ref.at[t],
            dst_ref=mrecv_ref.at[t],
            send_sem=msend_sem.at[t],
            recv_sem=mrecv_sem.at[t],
            device_id=(seq, mate),
            device_id_type=MESH,
        )

    def y_copy(t, k):
        return pltpu.make_async_remote_copy(
            src_ref=ysend_ref.at[t, k - 1],
            dst_ref=yrecv_ref.at[t, n_y - k - 1],
            send_sem=ysend_sem.at[t, k - 1],
            recv_sem=yrecv_sem.at[t, n_y - k - 1],
            device_id=(seq, y_peer(k) * 2 + core),
            device_id_type=MESH,
        )

    def pass_on(t):
        mate_copy(t).wait_recv()
        for k in range(1, n_y):
            ysend_ref[t, k - 1] = (
                own_ref[t, k].astype(jnp.float32) + mrecv_ref[t, k].astype(jnp.float32)
            ).astype(jnp.bfloat16)
            y_copy(t, k).start()

    def finish(t):
        total = own_ref[t, 0].astype(jnp.float32) + mrecv_ref[t, 0].astype(jnp.float32)
        for k in range(1, n_y):
            y_copy(t, k).wait_recv()
        for k in range(1, n_y):
            total = total + yrecv_ref[t, n_y - k - 1].astype(jnp.float32)
        out_ref[pl.ds(pl.multiple_of(t * proj_rows, proj_rows), proj_rows), :] = total.astype(
            jnp.bfloat16
        )
        mate_copy(t).wait_send()
        for k in range(1, n_y):
            y_copy(t, k).wait_send()

    def project(t):
        for k in range(n_y - 1, -1, -1):
            for target, dest in ((1 - core, msend_ref), (core, own_ref)):
                at = pl.multiple_of((y_peer(k) * 2 + target) * width, width)
                dest[t, k] = jnp.dot(
                    att_ref[...], w_ref[:, pl.ds(at, width)], preferred_element_type=jnp.float32
                ).astype(jnp.bfloat16)

    def chunk(t, carry):
        def part(i, c):
            local = i // kv_local
            attend(lax.rem(i, kv_local), t * per_chunk + local, local)

            @pl.when((i == 0) & (t > 0))
            def _():
                pass_on(t - 1)

            return c

        lax.fori_loop(0, per_chunk * kv_local, part, 0)

        @pl.when(t == 0)
        def _():
            w_copy.wait()

        @pl.when(t > 1)
        def _():
            finish(t - 2)

        project(t)
        mate_copy(t).start()
        return carry

    lax.fori_loop(0, chunks, chunk, 0)
    pass_on(chunks - 1)
    if chunks > 1:
        finish(chunks - 2)
    finish(chunks - 1)


def on_device(n_head, queries, keys, values, vertical_blocks, band_offsets, out_weight):
    tok_rows, heads_local, head_dim = queries.shape
    kv_local = keys.shape[1]
    group = heads_local // kv_local
    blocks = tok_rows // BLK
    list_len = vertical_blocks.shape[1]
    n_seq = lax.axis_size("seq")
    slot_cap = max(2, (list_len + n_seq - 2) // (n_seq - 1))
    slots = n_seq * slot_cap
    shard = lax.axis_index("seq")
    n_y = n_head // 2
    proj_rows = 2 * BLK
    chunks = tok_rows // proj_rows
    d_model = out_weight.shape[1]
    width = d_model // n_head

    pairs = [(i, i + 1) for i in range(n_seq - 1)]
    keys_h = jnp.swapaxes(keys, 0, 1)
    values_h = jnp.transpose(values, (1, 2, 0))
    kext = jnp.concatenate([lax.ppermute(keys_h, "seq", pairs), keys_h], axis=1)
    vext = jnp.concatenate([lax.ppermute(values_h, "seq", pairs), values_h], axis=2)
    owner = vertical_blocks // blocks
    entry = jnp.arange(list_len, dtype=jnp.int32)
    rank = jnp.sum(
        ((owner[:, :, None] == owner[:, None, :]) & (entry[None, None, :] < entry[None, :, None])).astype(
            jnp.int32
        ),
        axis=2,
    )
    where_slot = owner * slot_cap + rank
    slot_hit = where_slot[:, None, :] == jnp.arange(slots, dtype=jnp.int32)[None, :, None]
    slot_block = jnp.sum(jnp.where(slot_hit, vertical_blocks[:, None, :] + 1, 0), axis=2) - 1
    mine = lax.dynamic_slice_in_dim(slot_block, shard * slot_cap, slot_cap, 1)
    local_idx = jnp.where(mine >= 0, mine - shard * blocks, 0)
    key_blocks = keys_h.reshape(kv_local, blocks, BLK, head_dim)
    value_blocks = values_h.reshape(kv_local, head_dim, blocks, BLK)
    out_keys = jnp.stack([key_blocks[h][local_idx[h]] for h in range(kv_local)], axis=0)
    out_values = jnp.stack(
        [jnp.swapaxes(value_blocks[h][:, local_idx[h]], 0, 1) for h in range(kv_local)], axis=0
    )
    outgoing = jnp.stack([out_keys, out_values], axis=1)
    gathered = lax.all_gather(outgoing, "seq", axis=2, tiled=True)
    kslot = gathered[:, 0].reshape(kv_local, slots * BLK, head_dim)
    vslot = jnp.swapaxes(gathered[:, 1], 1, 2).reshape(kv_local, head_dim, slots * BLK)

    b_at = jnp.arange(blocks, dtype=jnp.int32)
    first = (shard - 1) * blocks + b_at
    slot_ok = (slot_block >= 0)[:, None, :] & (slot_block[:, None, :] < first[None, :, None])
    slot_bias = jnp.where(slot_ok, 0.0, MASKED).astype(jnp.float32).reshape(-1)
    w_at = jnp.arange(blocks + 1, dtype=jnp.int32)
    blk = first[:, None] + w_at[None, :]
    dist = blocks - w_at
    listed = jnp.any(blk[None, :, :, None] == vertical_blocks[:, None, None, :], axis=3)
    back = band_offsets // BLK
    on_low = jnp.any(back[:, None, :] == dist[None, :, None], axis=2)
    on_up = jnp.any(back[:, None, :] == dist[None, :, None] - 1, axis=2)
    low = (blk >= 0)[None] & (listed | on_low[:, None, :])
    up = ((blk >= 0) & (dist >= 1)[None, :])[None] & (listed | on_up[:, None, :])
    win_bias = jnp.where(jnp.stack([low, up], axis=2), 0.0, MASKED).astype(jnp.float32).reshape(-1)

    q = queries.reshape(blocks, BLK, kv_local, group, head_dim)
    q = jnp.transpose(q, (2, 0, 4, 3, 1)).reshape(kv_local, blocks, head_dim, group * BLK)

    vmem = pl.BlockSpec(memory_space=pltpu.VMEM)
    piece = (proj_rows, width)
    return pl.pallas_call(
        functools.partial(attend_kernel, n_head, slot_cap, proj_rows),
        out_shape=jax.ShapeDtypeStruct((tok_rows, width), jnp.bfloat16),
        in_specs=[vmem] * 5 + [pl.BlockSpec(memory_space=pltpu.SMEM)] * 2 + [pl.BlockSpec(memory_space=pl.ANY)],
        out_specs=vmem,
        scratch_shapes=[
            pltpu.VMEM(out_weight.shape, jnp.bfloat16),
            pltpu.VMEM((proj_rows, heads_local * head_dim), jnp.bfloat16),
            pltpu.VMEM((chunks, n_y) + piece, jnp.bfloat16),
            pltpu.VMEM((chunks, n_y) + piece, jnp.bfloat16),
            pltpu.VMEM((chunks, n_y) + piece, jnp.bfloat16),
            pltpu.VMEM((chunks, n_y - 1) + piece, jnp.bfloat16),
            pltpu.VMEM((chunks, n_y - 1) + piece, jnp.bfloat16),
            pltpu.SemaphoreType.DMA,
            pltpu.SemaphoreType.DMA((chunks,)),
            pltpu.SemaphoreType.DMA((chunks,)),
            pltpu.SemaphoreType.DMA((chunks, n_y - 1)),
            pltpu.SemaphoreType.DMA((chunks, n_y - 1)),
        ],
        compiler_params=pltpu.CompilerParams(
            collective_id=0, has_side_effects=True, vmem_limit_bytes=60 << 20
        ),
    )(
        q,
        kext,
        vext,
        kslot,
        vslot,
        win_bias,
        slot_bias,
        out_weight,
    )


def solution(mesh):
    return jax.shard_map(
        functools.partial(on_device, mesh.shape["head"]),
        mesh=mesh,
        in_specs=(
            P("seq", "head", None),
            P("seq", "head", None),
            P("seq", "head", None),
            P("head", None),
            P("head", None),
            P("head", None),
        ),
        out_specs=P("seq", "head"),
        check_vma=False,
    )
```

```python
import functools

import jax
import jax.numpy as jnp
from jax import lax
from jax.experimental import pallas as pl
from jax.experimental.pallas import tpu as pltpu
from jax.sharding import PartitionSpec as P

BLK = 128
MASKED = -1e30
MESH = pl.DeviceIdType.MESH
LOG2E = 1.4426950408889634

HALF = 2 * BLK


def peak(parts):
    most = parts[0]
    for part in parts[1:]:
        most = jnp.maximum(most, part)
    return jnp.max(most, axis=0, keepdims=True)


def weigh(parts, top, scale):
    weights = [jnp.exp2((part - top) * scale) for part in parts]
    total = weights[0]
    for weight in weights[1:]:
        total = total + weight
    probs = jnp.concatenate([weight.astype(jnp.bfloat16) for weight in weights], axis=0)
    return jnp.sum(total, axis=0, keepdims=True), probs


def window_kernel(q_ref, kext_ref, vext_ref, wbias_ref, top_ref, total_ref, acc_ref, s_ref):
    kv_local, blocks, head_dim, rows = q_ref.shape
    window = (blocks + 1) * BLK
    scale = head_dim ** (-0.5) * LOG2E
    halves = rows // HALF
    count = kv_local * blocks
    key_at = lax.broadcasted_iota(jnp.int32, (BLK, HALF), 0)
    query_at = lax.broadcasted_iota(jnp.int32, (BLK, HALF), 1) & (BLK - 1)
    lower = key_at <= query_at

    def scores(n, slot):
        h, b = n // blocks, lax.rem(n, blocks)
        start = pl.multiple_of(b * BLK, BLK)
        for i in range(halves):
            s_ref[slot, i] = jnp.dot(
                kext_ref[h, pl.ds(start, window), :],
                q_ref[h, b, :, i * HALF : (i + 1) * HALF],
                preferred_element_type=jnp.float32,
            )

    def absorb(n, slot):
        h, b = n // blocks, lax.rem(n, blocks)
        start = pl.multiple_of(b * BLK, BLK)
        at = n * (2 * (blocks + 1))
        biases = [
            jnp.where(lower, wbias_ref[at + w], wbias_ref[at + blocks + 1 + w])
            for w in range(blocks + 1)
        ]
        for i in range(halves):
            parts = [
                s_ref[slot, i, w * BLK : (w + 1) * BLK] + bias for w, bias in enumerate(biases)
            ]
            top = peak(parts)
            total, probs = weigh(parts, top, scale)
            lanes = slice(i * HALF, (i + 1) * HALF)
            top_ref[h, b, :, lanes] = top
            total_ref[h, b, :, lanes] = total
            acc_ref[h, b, :, lanes] = jnp.dot(
                vext_ref[h, :, pl.ds(start, window)], probs, preferred_element_type=jnp.float32
            )

    scores(0, 0)

    def two(nn, carry):
        n = nn * 2
        scores(n + 1, 1)
        absorb(n, 0)
        scores(lax.rem(n + 2, count), 0)
        absorb(n + 1, 1)
        return carry

    lax.fori_loop(0, count // 2, two, 0)


def attend_kernel(
    n_head,
    slot_cap,
    proj_rows,
    q_ref,
    top_ref,
    total_ref,
    acc_ref,
    kslot_ref,
    vslot_ref,
    sbias_ref,
    w_hbm,
    out_ref,
    s_ref,
    w_ref,
    att_ref,
    own_ref,
    msend_ref,
    mrecv_ref,
    ysend_ref,
    yrecv_ref,
    w_sem,
    msend_sem,
    mrecv_sem,
    ysend_sem,
    yrecv_sem,
):
    seq = lax.axis_index("seq")
    head = lax.axis_index("head")
    core = lax.rem(head, 2)
    y_at = head // 2
    n_y = n_head // 2
    mate = y_at * 2 + 1 - core
    kv_local, blocks, head_dim, rows = q_ref.shape
    slots = kslot_ref.shape[1] // BLK
    steps = slots // slot_cap
    group = rows // BLK
    step_keys = slot_cap * BLK
    width = w_ref.shape[1] // n_head
    chunks = blocks * BLK // proj_rows
    per_chunk = proj_rows // BLK
    scale = head_dim ** (-0.5) * LOG2E

    def y_peer(k):
        return lax.rem(y_at + k, n_y)

    w_copy = pltpu.make_async_copy(w_hbm, w_ref, w_sem)
    w_copy.start()
    barrier = pltpu.get_barrier_semaphore()
    pl.semaphore_signal(barrier, inc=1, device_id=(seq, mate), device_id_type=MESH)
    for k in range(1, n_y):
        pl.semaphore_signal(
            barrier, inc=1, device_id=(seq, y_peer(k) * 2 + core), device_id_type=MESH
        )
    pl.semaphore_wait(barrier, n_y)

    halves = rows // HALF

    def scores(h, b, j, slot):
        at = pl.multiple_of(j * step_keys, step_keys)
        for i in range(halves):
            s_ref[slot, i] = jnp.dot(
                kslot_ref[h, pl.ds(at, step_keys), :],
                q_ref[h, b, :, i * HALF : (i + 1) * HALF],
                preferred_element_type=jnp.float32,
            )

    def absorb(h, b, j, slot, running):
        at = pl.multiple_of(j * step_keys, step_keys)
        at_s = (h * blocks + b) * slots + j * slot_cap
        after = []
        for i, (top, total, acc) in enumerate(running):
            parts = [
                s_ref[slot, i, r * BLK : (r + 1) * BLK] + sbias_ref[at_s + r]
                for r in range(slot_cap)
            ]
            new_top = jnp.maximum(top, peak(parts))
            rescale = jnp.exp2((top - new_top) * scale)
            part_sum, probs = weigh(parts, new_top, scale)
            acc = acc * rescale + jnp.dot(
                vslot_ref[h, :, pl.ds(at, step_keys)], probs, preferred_element_type=jnp.float32
            )
            after.append((new_top, total * rescale + part_sum, acc))
        return tuple(after)

    def attend(h, b, local):
        scores(h, b, 0, 0)
        running = tuple(
            (
                top_ref[h, b, :, i * HALF : (i + 1) * HALF],
                total_ref[h, b, :, i * HALF : (i + 1) * HALF],
                acc_ref[h, b, :, i * HALF : (i + 1) * HALF],
            )
            for i in range(halves)
        )

        def two(jj, running):
            j = jj * 2
            scores(h, b, j + 1, 1)
            running = absorb(h, b, j, 0, running)
            scores(h, b, jnp.minimum(j + 2, steps - 1), 0)
            return absorb(h, b, j + 1, 1, running)

        running = lax.fori_loop(0, seq // 2, two, running)
        running = lax.fori_loop(
            0, lax.rem(seq, 2), lambda _, r: absorb(h, b, seq - 1, 0, r), running
        )
        for i, (_, total, acc) in enumerate(running):
            normed = acc / total
            for g in range(2):
                at = pl.multiple_of((h * group + 2 * i + g) * head_dim, head_dim)
                att_ref[pl.ds(local * BLK, BLK), pl.ds(at, head_dim)] = jnp.transpose(
                    normed[:, g * BLK : (g + 1) * BLK]
                ).astype(jnp.bfloat16)

    def mate_copy(t):
        return pltpu.make_async_remote_copy(
            src_ref=msend_ref.at[t],
            dst_ref=mrecv_ref.at[t],
            send_sem=msend_sem.at[t],
            recv_sem=mrecv_sem.at[t],
            device_id=(seq, mate),
            device_id_type=MESH,
        )

    def y_copy(t, k):
        return pltpu.make_async_remote_copy(
            src_ref=ysend_ref.at[t, k - 1],
            dst_ref=yrecv_ref.at[t, n_y - k - 1],
            send_sem=ysend_sem.at[t, k - 1],
            recv_sem=yrecv_sem.at[t, n_y - k - 1],
            device_id=(seq, y_peer(k) * 2 + core),
            device_id_type=MESH,
        )

    def pass_on(t):
        mate_copy(t).wait_recv()
        for k in range(1, n_y):
            ysend_ref[t, k - 1] = (
                own_ref[t, k].astype(jnp.float32) + mrecv_ref[t, k].astype(jnp.float32)
            ).astype(jnp.bfloat16)
            y_copy(t, k).start()

    def finish(t):
        total = own_ref[t, 0].astype(jnp.float32) + mrecv_ref[t, 0].astype(jnp.float32)
        for k in range(1, n_y):
            y_copy(t, k).wait_recv()
        for k in range(1, n_y):
            total = total + yrecv_ref[t, n_y - k - 1].astype(jnp.float32)
        out_ref[pl.ds(pl.multiple_of(t * proj_rows, proj_rows), proj_rows), :] = total.astype(
            jnp.bfloat16
        )
        mate_copy(t).wait_send()
        for k in range(1, n_y):
            y_copy(t, k).wait_send()

    def project(t):
        for k in range(n_y - 1, -1, -1):
            for target, dest in ((1 - core, msend_ref), (core, own_ref)):
                at = pl.multiple_of((y_peer(k) * 2 + target) * width, width)
                dest[t, k] = jnp.dot(
                    att_ref[...], w_ref[:, pl.ds(at, width)], preferred_element_type=jnp.float32
                ).astype(jnp.bfloat16)

    def chunk(t, carry):
        def part(i, c):
            local = i // kv_local
            attend(lax.rem(i, kv_local), t * per_chunk + local, local)

            @pl.when((i == 0) & (t > 0))
            def _():
                pass_on(t - 1)

            return c

        lax.fori_loop(0, per_chunk * kv_local, part, 0)

        @pl.when(t == 0)
        def _():
            w_copy.wait()

        @pl.when(t > 1)
        def _():
            finish(t - 2)

        project(t)
        mate_copy(t).start()
        return carry

    lax.fori_loop(0, chunks, chunk, 0)
    pass_on(chunks - 1)
    if chunks > 1:
        finish(chunks - 2)
    finish(chunks - 1)


def on_device(n_head, queries, keys, values, vertical_blocks, band_offsets, out_weight):
    tok_rows, heads_local, head_dim = queries.shape
    kv_local = keys.shape[1]
    group = heads_local // kv_local
    blocks = tok_rows // BLK
    list_len = vertical_blocks.shape[1]
    n_seq = lax.axis_size("seq")
    slot_cap = max(2, (list_len + n_seq - 2) // (n_seq - 1))
    slots = n_seq * slot_cap
    shard = lax.axis_index("seq")
    n_y = n_head // 2
    proj_rows = 2 * BLK
    chunks = tok_rows // proj_rows
    d_model = out_weight.shape[1]
    width = d_model // n_head

    pairs = [(i, i + 1) for i in range(n_seq - 1)]
    keys_h = jnp.swapaxes(keys, 0, 1)
    values_h = jnp.transpose(values, (1, 2, 0))
    kext = jnp.concatenate([lax.ppermute(keys_h, "seq", pairs), keys_h], axis=1)
    vext = jnp.concatenate([lax.ppermute(values_h, "seq", pairs), values_h], axis=2)
    owner = vertical_blocks // blocks
    entry = jnp.arange(list_len, dtype=jnp.int32)
    rank = jnp.sum(
        ((owner[:, :, None] == owner[:, None, :]) & (entry[None, None, :] < entry[None, :, None])).astype(
            jnp.int32
        ),
        axis=2,
    )
    where_slot = owner * slot_cap + rank
    slot_hit = where_slot[:, None, :] == jnp.arange(slots, dtype=jnp.int32)[None, :, None]
    slot_block = jnp.sum(jnp.where(slot_hit, vertical_blocks[:, None, :] + 1, 0), axis=2) - 1
    mine = lax.dynamic_slice_in_dim(slot_block, shard * slot_cap, slot_cap, 1)
    local_idx = jnp.where(mine >= 0, mine - shard * blocks, 0)
    key_blocks = keys_h.reshape(kv_local, blocks, BLK, head_dim)
    value_blocks = values_h.reshape(kv_local, head_dim, blocks, BLK)
    out_keys = jnp.stack([key_blocks[h][local_idx[h]] for h in range(kv_local)], axis=0)
    out_values = jnp.stack(
        [jnp.swapaxes(value_blocks[h][:, local_idx[h]], 0, 1) for h in range(kv_local)], axis=0
    )
    outgoing = jnp.stack([out_keys, out_values], axis=1)
    gathered = lax.all_gather(outgoing, "seq", axis=2, tiled=True)
    kslot = gathered[:, 0].reshape(kv_local, slots * BLK, head_dim)
    vslot = jnp.swapaxes(gathered[:, 1], 1, 2).reshape(kv_local, head_dim, slots * BLK)

    b_at = jnp.arange(blocks, dtype=jnp.int32)
    first = (shard - 1) * blocks + b_at
    slot_ok = (slot_block >= 0)[:, None, :] & (slot_block[:, None, :] < first[None, :, None])
    slot_bias = jnp.where(slot_ok, 0.0, MASKED).astype(jnp.float32).reshape(-1)
    w_at = jnp.arange(blocks + 1, dtype=jnp.int32)
    blk = first[:, None] + w_at[None, :]
    dist = blocks - w_at
    listed = jnp.any(blk[None, :, :, None] == vertical_blocks[:, None, None, :], axis=3)
    back = band_offsets // BLK
    on_low = jnp.any(back[:, None, :] == dist[None, :, None], axis=2)
    on_up = jnp.any(back[:, None, :] == dist[None, :, None] - 1, axis=2)
    low = (blk >= 0)[None] & (listed | on_low[:, None, :])
    up = ((blk >= 0) & (dist >= 1)[None, :])[None] & (listed | on_up[:, None, :])
    win_bias = jnp.where(jnp.stack([low, up], axis=2), 0.0, MASKED).astype(jnp.float32).reshape(-1)

    q = queries.reshape(blocks, BLK, kv_local, group, head_dim)
    q = jnp.transpose(q, (2, 0, 4, 3, 1)).reshape(kv_local, blocks, head_dim, group * BLK)

    vmem = pl.BlockSpec(memory_space=pltpu.VMEM)
    smem = pl.BlockSpec(memory_space=pltpu.SMEM)
    rows = group * BLK
    window = (blocks + 1) * BLK
    pairs_seen = kv_local * blocks * rows * window
    top, total, acc = pl.pallas_call(
        window_kernel,
        out_shape=[
            jax.ShapeDtypeStruct((kv_local, blocks, 1, rows), jnp.float32),
            jax.ShapeDtypeStruct((kv_local, blocks, 1, rows), jnp.float32),
            jax.ShapeDtypeStruct((kv_local, blocks, head_dim, rows), jnp.float32),
        ],
        in_specs=[vmem] * 3 + [smem],
        out_specs=[vmem] * 3,
        scratch_shapes=[pltpu.VMEM((2, rows // HALF, window, HALF), jnp.float32)],
        compiler_params=pltpu.CompilerParams(vmem_limit_bytes=32 << 20),
        cost_estimate=pl.CostEstimate(
            flops=8 * pairs_seen * head_dim, transcendentals=pairs_seen, bytes_accessed=10 << 20
        ),
    )(q, kext, vext, win_bias)
    piece = (proj_rows, width)
    return pl.pallas_call(
        functools.partial(attend_kernel, n_head, slot_cap, proj_rows),
        out_shape=jax.ShapeDtypeStruct((tok_rows, width), jnp.bfloat16),
        in_specs=[vmem] * 6 + [smem] + [pl.BlockSpec(memory_space=pl.ANY)],
        out_specs=vmem,
        scratch_shapes=[
            pltpu.VMEM((2, rows // HALF, slot_cap * BLK, HALF), jnp.float32),
            pltpu.VMEM(out_weight.shape, jnp.bfloat16),
            pltpu.VMEM((proj_rows, heads_local * head_dim), jnp.bfloat16),
            pltpu.VMEM((chunks, n_y) + piece, jnp.bfloat16),
            pltpu.VMEM((chunks, n_y) + piece, jnp.bfloat16),
            pltpu.VMEM((chunks, n_y) + piece, jnp.bfloat16),
            pltpu.VMEM((chunks, n_y - 1) + piece, jnp.bfloat16),
            pltpu.VMEM((chunks, n_y - 1) + piece, jnp.bfloat16),
            pltpu.SemaphoreType.DMA,
            pltpu.SemaphoreType.DMA((chunks,)),
            pltpu.SemaphoreType.DMA((chunks,)),
            pltpu.SemaphoreType.DMA((chunks, n_y - 1)),
            pltpu.SemaphoreType.DMA((chunks, n_y - 1)),
        ],
        compiler_params=pltpu.CompilerParams(
            collective_id=0, has_side_effects=True, vmem_limit_bytes=60 << 20
        ),
    )(
        q,
        top,
        total,
        acc,
        kslot,
        vslot,
        slot_bias,
        out_weight,
    )


def solution(mesh):
    return jax.shard_map(
        functools.partial(on_device, mesh.shape["head"]),
        mesh=mesh,
        in_specs=(
            P("seq", "head", None),
            P("seq", "head", None),
            P("seq", "head", None),
            P("head", None),
            P("head", None),
            P("head", None),
        ),
        out_specs=P("seq", "head"),
        check_vma=False,
    )
```

```python
import functools

import jax
import jax.numpy as jnp
from jax import lax
from jax.experimental import pallas as pl
from jax.experimental.pallas import tpu as pltpu
from jax.sharding import PartitionSpec as P

BLK = 128
MASKED = -1e30
MESH = pl.DeviceIdType.MESH
LOG2E = 1.4426950408889634

HALF = 2 * BLK


def peak(parts):
    most = parts[0]
    for part in parts[1:]:
        most = jnp.maximum(most, part)
    return jnp.max(most, axis=0, keepdims=True)


def weigh(parts, top, scale):
    weights = [jnp.exp2((part - top) * scale) for part in parts]
    total = weights[0]
    for weight in weights[1:]:
        total = total + weight
    probs = jnp.concatenate([weight.astype(jnp.bfloat16) for weight in weights], axis=0)
    return jnp.sum(total, axis=0, keepdims=True), probs


def window_kernel(q_ref, kext_ref, vext_ref, wbias_ref, top_ref, total_ref, acc_ref, s_ref):
    kv_local, blocks, head_dim, rows = q_ref.shape
    window = (blocks + 1) * BLK
    scale = head_dim ** (-0.5) * LOG2E
    halves = rows // HALF
    count = kv_local * blocks
    key_at = lax.broadcasted_iota(jnp.int32, (BLK, HALF), 0)
    query_at = lax.broadcasted_iota(jnp.int32, (BLK, HALF), 1) & (BLK - 1)
    lower = key_at <= query_at

    def scores(n, slot):
        h, b = n // blocks, lax.rem(n, blocks)
        start = pl.multiple_of(b * BLK, BLK)
        for i in range(halves):
            s_ref[slot, i] = jnp.dot(
                kext_ref[h, pl.ds(start, window), :],
                q_ref[h, b, :, i * HALF : (i + 1) * HALF],
                preferred_element_type=jnp.float32,
            )

    def absorb(n, slot):
        h, b = n // blocks, lax.rem(n, blocks)
        start = pl.multiple_of(b * BLK, BLK)
        at = n * (2 * (blocks + 1))
        biases = [
            jnp.where(lower, wbias_ref[at + w], wbias_ref[at + blocks + 1 + w])
            for w in range(blocks + 1)
        ]
        for i in range(halves):
            parts = [
                s_ref[slot, i, w * BLK : (w + 1) * BLK] + bias for w, bias in enumerate(biases)
            ]
            top = peak(parts)
            total, probs = weigh(parts, top, scale)
            lanes = slice(i * HALF, (i + 1) * HALF)
            top_ref[h, b, :, lanes] = top
            total_ref[h, b, :, lanes] = total
            acc_ref[h, b, :, lanes] = jnp.dot(
                vext_ref[h, :, pl.ds(start, window)], probs, preferred_element_type=jnp.float32
            )

    scores(0, 0)

    def two(nn, carry):
        n = nn * 2
        scores(n + 1, 1)
        absorb(n, 0)
        scores(lax.rem(n + 2, count), 0)
        absorb(n + 1, 1)
        return carry

    lax.fori_loop(0, count // 2, two, 0)


def listed_part(
    seq, slot_cap, h, q_ref, top_ref, total_ref, acc_ref, kslot_ref, vslot_ref, sbias_ref, s_ref, att_ref
):
    _, blocks, head_dim, rows = q_ref.shape
    slots = kslot_ref.shape[0] // BLK
    steps = slots // slot_cap
    step_keys = slot_cap * BLK
    scale = head_dim ** (-0.5) * LOG2E
    halves = rows // HALF

    def scores(b, j, slot):
        at = pl.multiple_of(j * step_keys, step_keys)
        for i in range(halves):
            s_ref[slot, i] = jnp.dot(
                kslot_ref[pl.ds(at, step_keys), :],
                q_ref[h, b, :, i * HALF : (i + 1) * HALF],
                preferred_element_type=jnp.float32,
            )

    def absorb(b, j, slot, running):
        at = pl.multiple_of(j * step_keys, step_keys)
        at_s = (h * blocks + b) * slots + j * slot_cap
        after = []
        for i, (top, total, acc) in enumerate(running):
            parts = [
                s_ref[slot, i, r * BLK : (r + 1) * BLK] + sbias_ref[at_s + r]
                for r in range(slot_cap)
            ]
            new_top = jnp.maximum(top, peak(parts))
            rescale = jnp.exp2((top - new_top) * scale)
            part_sum, probs = weigh(parts, new_top, scale)
            acc = acc * rescale + jnp.dot(
                vslot_ref[:, pl.ds(at, step_keys)], probs, preferred_element_type=jnp.float32
            )
            after.append((new_top, total * rescale + part_sum, acc))
        return tuple(after)

    def attend(b, row, lane):
        scores(b, 0, 0)
        running = tuple(
            (
                top_ref[h, b, :, i * HALF : (i + 1) * HALF],
                total_ref[h, b, :, i * HALF : (i + 1) * HALF],
                acc_ref[h, b, :, i * HALF : (i + 1) * HALF],
            )
            for i in range(halves)
        )

        def two(jj, running):
            j = jj * 2
            scores(b, j + 1, 1)
            running = absorb(b, j, 0, running)
            scores(b, jnp.minimum(j + 2, steps - 1), 0)
            return absorb(b, j + 1, 1, running)

        running = lax.fori_loop(0, seq // 2, two, running)
        running = lax.fori_loop(
            0, lax.rem(seq, 2), lambda _, r: absorb(b, seq - 1, 0, r), running
        )
        for i, (_, total, acc) in enumerate(running):
            normed = acc / total
            for g in range(2):
                at = lane + (2 * i + g) * head_dim
                att_ref[pl.ds(row, BLK), at : at + head_dim] = jnp.transpose(
                    normed[:, g * BLK : (g + 1) * BLK]
                ).astype(jnp.bfloat16)

    return attend


def early_kernel(
    slot_cap, early, q_ref, top_ref, total_ref, acc_ref, sbias_ref, *rest
):
    slot_refs, (att_ref, s_ref) = rest[: 2 * early], rest[2 * early :]
    seq = lax.axis_index("seq")
    _, blocks, head_dim, rows = q_ref.shape
    for h in range(early):
        attend = listed_part(
            seq,
            slot_cap,
            h,
            q_ref,
            top_ref,
            total_ref,
            acc_ref,
            slot_refs[2 * h],
            slot_refs[2 * h + 1],
            sbias_ref,
            s_ref,
            att_ref,
        )

        def block(b, carry):
            attend(b, pl.multiple_of(b * BLK, BLK), h * (rows // BLK) * head_dim)
            return carry

        lax.fori_loop(0, blocks, block, 0)


def attend_kernel(
    n_head,
    slot_cap,
    proj_rows,
    q_ref,
    top_ref,
    total_ref,
    acc_ref,
    kslot_ref,
    vslot_ref,
    sbias_ref,
    early_ref,
    w_hbm,
    out_ref,
    s_ref,
    w_ref,
    att_ref,
    own_ref,
    msend_ref,
    mrecv_ref,
    ysend_ref,
    yrecv_ref,
    w_sem,
    msend_sem,
    mrecv_sem,
    ysend_sem,
    yrecv_sem,
):
    seq = lax.axis_index("seq")
    head = lax.axis_index("head")
    core = lax.rem(head, 2)
    y_at = head // 2
    n_y = n_head // 2
    mate = y_at * 2 + 1 - core
    kv_local, blocks, head_dim, rows = q_ref.shape
    group = rows // BLK
    width = w_ref.shape[1] // n_head
    chunks = blocks * BLK // proj_rows
    per_chunk = proj_rows // BLK

    def y_peer(k):
        return lax.rem(y_at + k, n_y)

    w_copy = pltpu.make_async_copy(w_hbm, w_ref, w_sem)
    w_copy.start()
    barrier = pltpu.get_barrier_semaphore()
    pl.semaphore_signal(barrier, inc=1, device_id=(seq, mate), device_id_type=MESH)
    for k in range(1, n_y):
        pl.semaphore_signal(
            barrier, inc=1, device_id=(seq, y_peer(k) * 2 + core), device_id_type=MESH
        )
    pl.semaphore_wait(barrier, n_y)

    last = kv_local - 1
    early_width = last * group * head_dim
    attend = listed_part(
        seq,
        slot_cap,
        last,
        q_ref,
        top_ref,
        total_ref,
        acc_ref,
        kslot_ref,
        vslot_ref,
        sbias_ref,
        s_ref,
        att_ref,
    )

    def mate_copy(t):
        return pltpu.make_async_remote_copy(
            src_ref=msend_ref.at[t],
            dst_ref=mrecv_ref.at[t],
            send_sem=msend_sem.at[t],
            recv_sem=mrecv_sem.at[t],
            device_id=(seq, mate),
            device_id_type=MESH,
        )

    def y_copy(t, k):
        return pltpu.make_async_remote_copy(
            src_ref=ysend_ref.at[t, k - 1],
            dst_ref=yrecv_ref.at[t, n_y - k - 1],
            send_sem=ysend_sem.at[t, k - 1],
            recv_sem=yrecv_sem.at[t, n_y - k - 1],
            device_id=(seq, y_peer(k) * 2 + core),
            device_id_type=MESH,
        )

    def pass_on(t):
        mate_copy(t).wait_recv()
        for k in range(1, n_y):
            ysend_ref[t, k - 1] = (
                own_ref[t, k].astype(jnp.float32) + mrecv_ref[t, k].astype(jnp.float32)
            ).astype(jnp.bfloat16)
            y_copy(t, k).start()

    def finish(t):
        total = own_ref[t, 0].astype(jnp.float32) + mrecv_ref[t, 0].astype(jnp.float32)
        for k in range(1, n_y):
            y_copy(t, k).wait_recv()
        for k in range(1, n_y):
            total = total + yrecv_ref[t, n_y - k - 1].astype(jnp.float32)
        out_ref[pl.ds(pl.multiple_of(t * proj_rows, proj_rows), proj_rows), :] = total.astype(
            jnp.bfloat16
        )
        mate_copy(t).wait_send()
        for k in range(1, n_y):
            y_copy(t, k).wait_send()

    def project(t):
        for k in range(n_y - 1, -1, -1):
            for target, dest in ((1 - core, msend_ref), (core, own_ref)):
                at = pl.multiple_of((y_peer(k) * 2 + target) * width, width)
                dest[t, k] = jnp.dot(
                    att_ref[...], w_ref[:, pl.ds(at, width)], preferred_element_type=jnp.float32
                ).astype(jnp.bfloat16)

    def chunk(t, carry):
        def part(i, c):
            attend(t * per_chunk + i, pl.multiple_of(i * BLK, BLK), early_width)

            @pl.when((i == 0) & (t > 0))
            def _():
                pass_on(t - 1)

            return c

        lax.fori_loop(0, per_chunk, part, 0)
        if early_width:
            att_ref[:, :early_width] = early_ref[
                pl.ds(pl.multiple_of(t * proj_rows, proj_rows), proj_rows), :
            ]

        @pl.when(t == 0)
        def _():
            w_copy.wait()

        @pl.when(t > 1)
        def _():
            finish(t - 2)

        project(t)
        mate_copy(t).start()
        return carry

    lax.fori_loop(0, chunks, chunk, 0)
    pass_on(chunks - 1)
    if chunks > 1:
        finish(chunks - 2)
    finish(chunks - 1)


def on_device(n_head, queries, keys, values, vertical_blocks, band_offsets, out_weight):
    tok_rows, heads_local, head_dim = queries.shape
    kv_local = keys.shape[1]
    group = heads_local // kv_local
    blocks = tok_rows // BLK
    list_len = vertical_blocks.shape[1]
    n_seq = lax.axis_size("seq")
    slot_cap = max(2, (list_len + n_seq - 2) // (n_seq - 1))
    slots = n_seq * slot_cap
    shard = lax.axis_index("seq")
    n_y = n_head // 2
    proj_rows = 2 * BLK
    chunks = tok_rows // proj_rows
    d_model = out_weight.shape[1]
    width = d_model // n_head

    pairs = [(i, i + 1) for i in range(n_seq - 1)]
    keys_h = jnp.swapaxes(keys, 0, 1)
    values_h = jnp.transpose(values, (1, 2, 0))
    kext = jnp.concatenate([lax.ppermute(keys_h, "seq", pairs), keys_h], axis=1)
    vext = jnp.concatenate([lax.ppermute(values_h, "seq", pairs), values_h], axis=2)
    owner = vertical_blocks // blocks
    entry = jnp.arange(list_len, dtype=jnp.int32)
    rank = jnp.sum(
        ((owner[:, :, None] == owner[:, None, :]) & (entry[None, None, :] < entry[None, :, None])).astype(
            jnp.int32
        ),
        axis=2,
    )
    where_slot = owner * slot_cap + rank
    slot_hit = where_slot[:, None, :] == jnp.arange(slots, dtype=jnp.int32)[None, :, None]
    slot_block = jnp.sum(jnp.where(slot_hit, vertical_blocks[:, None, :] + 1, 0), axis=2) - 1
    mine = lax.dynamic_slice_in_dim(slot_block, shard * slot_cap, slot_cap, 1)
    local_idx = jnp.where(mine >= 0, mine - shard * blocks, 0)
    key_blocks = keys_h.reshape(kv_local, blocks, BLK, head_dim)
    value_blocks = values_h.reshape(kv_local, head_dim, blocks, BLK)
    out_keys = jnp.stack([key_blocks[h][local_idx[h]] for h in range(kv_local)], axis=0)
    out_values = jnp.stack(
        [jnp.swapaxes(value_blocks[h][:, local_idx[h]], 0, 1) for h in range(kv_local)], axis=0
    )
    slot_rows = []
    for h in range(kv_local):
        outgoing = jnp.stack([out_keys[h], out_values[h]], axis=0)
        if slot_rows:
            outgoing, slot_rows[-1] = lax.optimization_barrier((outgoing, slot_rows[-1]))
        slot_rows.append(lax.all_gather(outgoing, "seq", axis=1, tiled=True))
    kslot = [g[0].reshape(slots * BLK, head_dim) for g in slot_rows]
    vslot = [jnp.swapaxes(g[1], 0, 1).reshape(head_dim, slots * BLK) for g in slot_rows]

    b_at = jnp.arange(blocks, dtype=jnp.int32)
    first = (shard - 1) * blocks + b_at
    slot_ok = (slot_block >= 0)[:, None, :] & (slot_block[:, None, :] < first[None, :, None])
    slot_bias = jnp.where(slot_ok, 0.0, MASKED).astype(jnp.float32).reshape(-1)
    w_at = jnp.arange(blocks + 1, dtype=jnp.int32)
    blk = first[:, None] + w_at[None, :]
    dist = blocks - w_at
    listed = jnp.any(blk[None, :, :, None] == vertical_blocks[:, None, None, :], axis=3)
    back = band_offsets // BLK
    on_low = jnp.any(back[:, None, :] == dist[None, :, None], axis=2)
    on_up = jnp.any(back[:, None, :] == dist[None, :, None] - 1, axis=2)
    low = (blk >= 0)[None] & (listed | on_low[:, None, :])
    up = ((blk >= 0) & (dist >= 1)[None, :])[None] & (listed | on_up[:, None, :])
    win_bias = jnp.where(jnp.stack([low, up], axis=2), 0.0, MASKED).astype(jnp.float32).reshape(-1)

    q = queries.reshape(blocks, BLK, kv_local, group, head_dim)
    q = jnp.transpose(q, (2, 0, 4, 3, 1)).reshape(kv_local, blocks, head_dim, group * BLK)

    vmem = pl.BlockSpec(memory_space=pltpu.VMEM)
    smem = pl.BlockSpec(memory_space=pltpu.SMEM)
    rows = group * BLK
    window = (blocks + 1) * BLK
    pairs_seen = kv_local * blocks * rows * window
    top, total, acc = pl.pallas_call(
        window_kernel,
        out_shape=[
            jax.ShapeDtypeStruct((kv_local, blocks, 1, rows), jnp.float32),
            jax.ShapeDtypeStruct((kv_local, blocks, 1, rows), jnp.float32),
            jax.ShapeDtypeStruct((kv_local, blocks, head_dim, rows), jnp.float32),
        ],
        in_specs=[vmem] * 3 + [smem],
        out_specs=[vmem] * 3,
        scratch_shapes=[pltpu.VMEM((2, rows // HALF, window, HALF), jnp.float32)],
        compiler_params=pltpu.CompilerParams(vmem_limit_bytes=32 << 20),
        cost_estimate=pl.CostEstimate(
            flops=8 * pairs_seen * head_dim, transcendentals=pairs_seen, bytes_accessed=10 << 20
        ),
    )(q, kext, vext, win_bias)
    piece = (proj_rows, width)
    early = kv_local - 1
    step_scratch = pltpu.VMEM((2, rows // HALF, slot_cap * BLK, HALF), jnp.float32)
    if early:
        pairs_seen = early * blocks * rows * slots * BLK
        early_att = pl.pallas_call(
            functools.partial(early_kernel, slot_cap, early),
            out_shape=jax.ShapeDtypeStruct((tok_rows, early * group * head_dim), jnp.bfloat16),
            in_specs=[vmem] * 4 + [smem] + [vmem] * (2 * early),
            out_specs=vmem,
            scratch_shapes=[step_scratch],
            compiler_params=pltpu.CompilerParams(vmem_limit_bytes=32 << 20),
            cost_estimate=pl.CostEstimate(
                flops=8 * pairs_seen * head_dim, transcendentals=pairs_seen, bytes_accessed=10 << 20
            ),
        )(q, top, total, acc, slot_bias, *[x for h in range(early) for x in (kslot[h], vslot[h])])
    else:
        early_att = jnp.zeros((tok_rows, head_dim), jnp.bfloat16)
    return pl.pallas_call(
        functools.partial(attend_kernel, n_head, slot_cap, proj_rows),
        out_shape=jax.ShapeDtypeStruct((tok_rows, width), jnp.bfloat16),
        in_specs=[vmem] * 6 + [smem, vmem] + [pl.BlockSpec(memory_space=pl.ANY)],
        out_specs=vmem,
        scratch_shapes=[
            step_scratch,
            pltpu.VMEM(out_weight.shape, jnp.bfloat16),
            pltpu.VMEM((proj_rows, heads_local * head_dim), jnp.bfloat16),
            pltpu.VMEM((chunks, n_y) + piece, jnp.bfloat16),
            pltpu.VMEM((chunks, n_y) + piece, jnp.bfloat16),
            pltpu.VMEM((chunks, n_y) + piece, jnp.bfloat16),
            pltpu.VMEM((chunks, n_y - 1) + piece, jnp.bfloat16),
            pltpu.VMEM((chunks, n_y - 1) + piece, jnp.bfloat16),
            pltpu.SemaphoreType.DMA,
            pltpu.SemaphoreType.DMA((chunks,)),
            pltpu.SemaphoreType.DMA((chunks,)),
            pltpu.SemaphoreType.DMA((chunks, n_y - 1)),
            pltpu.SemaphoreType.DMA((chunks, n_y - 1)),
        ],
        compiler_params=pltpu.CompilerParams(
            collective_id=0, has_side_effects=True, vmem_limit_bytes=60 << 20
        ),
    )(
        q,
        top,
        total,
        acc,
        kslot[-1],
        vslot[-1],
        slot_bias,
        early_att,
        out_weight,
    )


def solution(mesh):
    return jax.shard_map(
        functools.partial(on_device, mesh.shape["head"]),
        mesh=mesh,
        in_specs=(
            P("seq", "head", None),
            P("seq", "head", None),
            P("seq", "head", None),
            P("head", None),
            P("head", None),
            P("head", None),
        ),
        out_specs=P("seq", "head"),
        check_vma=False,
    )
```

```python
import functools

import jax
import jax.numpy as jnp
from jax import lax
from jax.experimental import pallas as pl
from jax.experimental.pallas import tpu as pltpu
from jax.sharding import PartitionSpec as P

BLK = 128
MASKED = -1e30
MESH = pl.DeviceIdType.MESH
LOG2E = 1.4426950408889634

HALF = 2 * BLK


def peak(parts):
    most = parts[0]
    for part in parts[1:]:
        most = jnp.maximum(most, part)
    return jnp.max(most, axis=0, keepdims=True)


def weigh(parts, top, scale):
    weights = [jnp.exp2((part - top) * scale) for part in parts]
    total = weights[0]
    for weight in weights[1:]:
        total = total + weight
    probs = jnp.concatenate([weight.astype(jnp.bfloat16) for weight in weights], axis=0)
    return jnp.sum(total, axis=0, keepdims=True), probs


def window_kernel(q_ref, kext_ref, vext_ref, wbias_ref, top_ref, total_ref, acc_ref, s_ref):
    kv_local, blocks, head_dim, rows = q_ref.shape
    window = (blocks + 1) * BLK
    scale = head_dim ** (-0.5) * LOG2E
    halves = rows // HALF
    count = kv_local * blocks
    key_at = lax.broadcasted_iota(jnp.int32, (BLK, HALF), 0)
    query_at = lax.broadcasted_iota(jnp.int32, (BLK, HALF), 1) & (BLK - 1)
    lower = key_at <= query_at

    def scores(n, slot):
        h, b = n // blocks, lax.rem(n, blocks)
        start = pl.multiple_of(b * BLK, BLK)
        for i in range(halves):
            s_ref[slot, i] = jnp.dot(
                kext_ref[h, pl.ds(start, window), :],
                q_ref[h, b, :, i * HALF : (i + 1) * HALF],
                preferred_element_type=jnp.float32,
            )

    def absorb(n, slot):
        h, b = n // blocks, lax.rem(n, blocks)
        start = pl.multiple_of(b * BLK, BLK)
        at = n * (2 * (blocks + 1))
        biases = [
            jnp.where(lower, wbias_ref[at + w], wbias_ref[at + blocks + 1 + w])
            for w in range(blocks + 1)
        ]
        for i in range(halves):
            parts = [
                s_ref[slot, i, w * BLK : (w + 1) * BLK] + bias for w, bias in enumerate(biases)
            ]
            top = peak(parts)
            total, probs = weigh(parts, top, scale)
            lanes = slice(i * HALF, (i + 1) * HALF)
            top_ref[h, b, :, lanes] = top
            total_ref[h, b, :, lanes] = total
            acc_ref[h, b, :, lanes] = jnp.dot(
                vext_ref[h, :, pl.ds(start, window)], probs, preferred_element_type=jnp.float32
            )

    scores(0, 0)

    def two(nn, carry):
        n = nn * 2
        scores(n + 1, 1)
        absorb(n, 0)
        scores(lax.rem(n + 2, count), 0)
        absorb(n + 1, 1)
        return carry

    lax.fori_loop(0, count // 2, two, 0)


def listed_part(
    seq, slot_cap, h, q_ref, top_ref, total_ref, acc_ref, kslot_ref, vslot_ref, sbias_ref, s_ref, att_ref
):
    _, blocks, head_dim, rows = q_ref.shape
    slots = kslot_ref.shape[0] // BLK
    steps = slots // slot_cap
    step_keys = slot_cap * BLK
    scale = head_dim ** (-0.5) * LOG2E
    halves = rows // HALF

    def scores(b, j, slot):
        at = pl.multiple_of(j * step_keys, step_keys)
        for i in range(halves):
            s_ref[slot, i] = jnp.dot(
                kslot_ref[pl.ds(at, step_keys), :],
                q_ref[h, b, :, i * HALF : (i + 1) * HALF],
                preferred_element_type=jnp.float32,
            )

    def absorb(b, j, slot, running):
        at = pl.multiple_of(j * step_keys, step_keys)
        at_s = (h * blocks + b) * slots + j * slot_cap
        after = []
        for i, (top, total, acc) in enumerate(running):
            parts = [
                s_ref[slot, i, r * BLK : (r + 1) * BLK] + sbias_ref[at_s + r]
                for r in range(slot_cap)
            ]
            new_top = jnp.maximum(top, peak(parts))
            rescale = jnp.exp2((top - new_top) * scale)
            part_sum, probs = weigh(parts, new_top, scale)
            acc = acc * rescale + jnp.dot(
                vslot_ref[:, pl.ds(at, step_keys)], probs, preferred_element_type=jnp.float32
            )
            after.append((new_top, total * rescale + part_sum, acc))
        return tuple(after)

    def attend(b, row, lane):
        scores(b, 0, 0)
        running = tuple(
            (
                top_ref[h, b, :, i * HALF : (i + 1) * HALF],
                total_ref[h, b, :, i * HALF : (i + 1) * HALF],
                acc_ref[h, b, :, i * HALF : (i + 1) * HALF],
            )
            for i in range(halves)
        )

        def two(jj, running):
            j = jj * 2
            scores(b, j + 1, 1)
            running = absorb(b, j, 0, running)
            scores(b, jnp.minimum(j + 2, steps - 1), 0)
            return absorb(b, j + 1, 1, running)

        running = lax.fori_loop(0, seq // 2, two, running)
        running = lax.fori_loop(
            0, lax.rem(seq, 2), lambda _, r: absorb(b, seq - 1, 0, r), running
        )
        for i, (_, total, acc) in enumerate(running):
            normed = acc / total
            for g in range(2):
                at = lane + (2 * i + g) * head_dim
                att_ref[pl.ds(row, BLK), at : at + head_dim] = jnp.transpose(
                    normed[:, g * BLK : (g + 1) * BLK]
                ).astype(jnp.bfloat16)

    return attend


def early_kernel(
    slot_cap, early, q_ref, top_ref, total_ref, acc_ref, sbias_ref, *rest
):
    slot_refs, (att_ref, s_ref) = rest[: 2 * early], rest[2 * early :]
    seq = lax.axis_index("seq")
    _, blocks, head_dim, rows = q_ref.shape
    for h in range(early):
        attend = listed_part(
            seq,
            slot_cap,
            h,
            q_ref,
            top_ref,
            total_ref,
            acc_ref,
            slot_refs[2 * h],
            slot_refs[2 * h + 1],
            sbias_ref,
            s_ref,
            att_ref,
        )

        def block(b, carry):
            attend(b, pl.multiple_of(b * BLK, BLK), h * (rows // BLK) * head_dim)
            return carry

        lax.fori_loop(0, blocks, block, 0)


def attend_kernel(
    n_head,
    slot_cap,
    proj_rows,
    q_ref,
    top_ref,
    total_ref,
    acc_ref,
    kslot_ref,
    vslot_ref,
    sbias_ref,
    early_ref,
    w_hbm,
    out_ref,
    s_ref,
    w_ref,
    att_ref,
    own_ref,
    msend_ref,
    mrecv_ref,
    ysend_ref,
    yrecv_ref,
    w_sem,
    msend_sem,
    mrecv_sem,
    ysend_sem,
    yrecv_sem,
):
    seq = lax.axis_index("seq")
    head = lax.axis_index("head")
    core = lax.rem(head, 2)
    y_at = head // 2
    n_y = n_head // 2
    mate = y_at * 2 + 1 - core
    kv_local, blocks, head_dim, rows = q_ref.shape
    group = rows // BLK
    width = w_ref.shape[1] // n_head
    chunks = blocks * BLK // proj_rows
    per_chunk = proj_rows // BLK

    def y_peer(k):
        return lax.rem(y_at + k, n_y)

    w_copy = pltpu.make_async_copy(w_hbm, w_ref, w_sem)
    w_copy.start()
    barrier = pltpu.get_barrier_semaphore()
    pl.semaphore_signal(barrier, inc=1, device_id=(seq, mate), device_id_type=MESH)
    for k in range(1, n_y):
        pl.semaphore_signal(
            barrier, inc=1, device_id=(seq, y_peer(k) * 2 + core), device_id_type=MESH
        )
    pl.semaphore_wait(barrier, n_y)

    last = kv_local - 1
    early_width = last * group * head_dim
    attend = listed_part(
        seq,
        slot_cap,
        last,
        q_ref,
        top_ref,
        total_ref,
        acc_ref,
        kslot_ref,
        vslot_ref,
        sbias_ref,
        s_ref,
        att_ref,
    )

    def mate_copy(t):
        return pltpu.make_async_remote_copy(
            src_ref=msend_ref.at[t],
            dst_ref=mrecv_ref.at[t],
            send_sem=msend_sem.at[t],
            recv_sem=mrecv_sem.at[t],
            device_id=(seq, mate),
            device_id_type=MESH,
        )

    def y_copy(t, k):
        return pltpu.make_async_remote_copy(
            src_ref=ysend_ref.at[t, k - 1],
            dst_ref=yrecv_ref.at[t, n_y - k - 1],
            send_sem=ysend_sem.at[t, k - 1],
            recv_sem=yrecv_sem.at[t, n_y - k - 1],
            device_id=(seq, y_peer(k) * 2 + core),
            device_id_type=MESH,
        )

    def pass_on(t):
        mate_copy(t).wait_recv()
        for k in range(1, n_y):
            ysend_ref[t, k - 1] = (
                own_ref[t, k].astype(jnp.float32) + mrecv_ref[t, k].astype(jnp.float32)
            ).astype(jnp.bfloat16)
            y_copy(t, k).start()

    def finish(t):
        total = own_ref[t, 0].astype(jnp.float32) + mrecv_ref[t, 0].astype(jnp.float32)
        for k in range(1, n_y):
            y_copy(t, k).wait_recv()
        for k in range(1, n_y):
            total = total + yrecv_ref[t, n_y - k - 1].astype(jnp.float32)
        out_ref[pl.ds(pl.multiple_of(t * proj_rows, proj_rows), proj_rows), :] = total.astype(
            jnp.bfloat16
        )
        mate_copy(t).wait_send()
        for k in range(1, n_y):
            y_copy(t, k).wait_send()

    def project(t):
        for k in range(n_y - 1, -1, -1):
            for target, dest in ((1 - core, msend_ref), (core, own_ref)):
                at = pl.multiple_of((y_peer(k) * 2 + target) * width, width)
                dest[t, k] = jnp.dot(
                    att_ref[...], w_ref[:, pl.ds(at, width)], preferred_element_type=jnp.float32
                ).astype(jnp.bfloat16)

    def chunk(t, carry):
        def part(i, c):
            attend(t * per_chunk + i, pl.multiple_of(i * BLK, BLK), early_width)

            @pl.when((i == 0) & (t > 0))
            def _():
                pass_on(t - 1)

            return c

        lax.fori_loop(0, per_chunk, part, 0)
        if early_width:
            att_ref[:, :early_width] = early_ref[
                pl.ds(pl.multiple_of(t * proj_rows, proj_rows), proj_rows), :
            ]

        @pl.when(t == 0)
        def _():
            w_copy.wait()

        @pl.when(t > 1)
        def _():
            finish(t - 2)

        project(t)
        mate_copy(t).start()
        return carry

    lax.fori_loop(0, chunks, chunk, 0)
    pass_on(chunks - 1)
    if chunks > 1:
        finish(chunks - 2)
    finish(chunks - 1)


def on_device(n_head, queries, keys, values, vertical_blocks, band_offsets, out_weight):
    tok_rows, heads_local, head_dim = queries.shape
    kv_local = keys.shape[1]
    group = heads_local // kv_local
    blocks = tok_rows // BLK
    list_len = vertical_blocks.shape[1]
    n_seq = lax.axis_size("seq")
    slot_cap = max(2, (list_len + n_seq - 2) // (n_seq - 1))
    slots = n_seq * slot_cap
    shard = lax.axis_index("seq")
    n_y = n_head // 2
    proj_rows = 2 * BLK
    chunks = tok_rows // proj_rows
    d_model = out_weight.shape[1]
    width = d_model // n_head

    pairs = [(i, i + 1) for i in range(n_seq - 1)]
    keys_h = jnp.swapaxes(keys, 0, 1)
    values_h = jnp.transpose(values, (1, 2, 0))
    kext = jnp.concatenate([lax.ppermute(keys_h, "seq", pairs), keys_h], axis=1)
    vext = jnp.concatenate([lax.ppermute(values_h, "seq", pairs), values_h], axis=2)
    owner = vertical_blocks // blocks
    entry = jnp.arange(list_len, dtype=jnp.int32)
    rank = jnp.sum(
        ((owner[:, :, None] == owner[:, None, :]) & (entry[None, None, :] < entry[None, :, None])).astype(
            jnp.int32
        ),
        axis=2,
    )
    where_slot = owner * slot_cap + rank
    slot_hit = where_slot[:, None, :] == jnp.arange(slots, dtype=jnp.int32)[None, :, None]
    slot_block = jnp.sum(jnp.where(slot_hit, vertical_blocks[:, None, :] + 1, 0), axis=2) - 1
    mine = lax.dynamic_slice_in_dim(slot_block, shard * slot_cap, slot_cap, 1)
    local_idx = jnp.where(mine >= 0, mine - shard * blocks, 0)
    key_blocks = keys_h.reshape(kv_local, blocks, BLK, head_dim)
    value_blocks = values_h.reshape(kv_local, head_dim, blocks, BLK)
    out_keys = jnp.stack([key_blocks[h][local_idx[h]] for h in range(kv_local)], axis=0)
    out_values = jnp.stack(
        [jnp.swapaxes(value_blocks[h][:, local_idx[h]], 0, 1) for h in range(kv_local)], axis=0
    )
    b_at = jnp.arange(blocks, dtype=jnp.int32)
    first = (shard - 1) * blocks + b_at
    slot_ok = (slot_block >= 0)[:, None, :] & (slot_block[:, None, :] < first[None, :, None])
    slot_bias = jnp.where(slot_ok, 0.0, MASKED).astype(jnp.float32).reshape(-1)
    w_at = jnp.arange(blocks + 1, dtype=jnp.int32)
    blk = first[:, None] + w_at[None, :]
    dist = blocks - w_at
    listed = jnp.any(blk[None, :, :, None] == vertical_blocks[:, None, None, :], axis=3)
    back = band_offsets // BLK
    on_low = jnp.any(back[:, None, :] == dist[None, :, None], axis=2)
    on_up = jnp.any(back[:, None, :] == dist[None, :, None] - 1, axis=2)
    low = (blk >= 0)[None] & (listed | on_low[:, None, :])
    up = ((blk >= 0) & (dist >= 1)[None, :])[None] & (listed | on_up[:, None, :])
    win_bias = jnp.where(jnp.stack([low, up], axis=2), 0.0, MASKED).astype(jnp.float32).reshape(-1)

    q = queries.reshape(blocks, BLK, kv_local, group, head_dim)
    q = jnp.transpose(q, (2, 0, 4, 3, 1)).reshape(kv_local, blocks, head_dim, group * BLK)

    vmem = pl.BlockSpec(memory_space=pltpu.VMEM)
    smem = pl.BlockSpec(memory_space=pltpu.SMEM)
    rows = group * BLK
    window = (blocks + 1) * BLK
    pairs_seen = kv_local * blocks * rows * window
    top, total, acc = pl.pallas_call(
        window_kernel,
        out_shape=[
            jax.ShapeDtypeStruct((kv_local, blocks, 1, rows), jnp.float32),
            jax.ShapeDtypeStruct((kv_local, blocks, 1, rows), jnp.float32),
            jax.ShapeDtypeStruct((kv_local, blocks, head_dim, rows), jnp.float32),
        ],
        in_specs=[vmem] * 3 + [smem],
        out_specs=[vmem] * 3,
        scratch_shapes=[pltpu.VMEM((2, rows // HALF, window, HALF), jnp.float32)],
        compiler_params=pltpu.CompilerParams(vmem_limit_bytes=32 << 20),
        cost_estimate=pl.CostEstimate(
            flops=8 * pairs_seen * head_dim, transcendentals=pairs_seen, bytes_accessed=10 << 20
        ),
    )(q, kext, vext, win_bias)
    slot_rows = []
    for h in range(kv_local):
        outgoing = jnp.stack([out_keys[h], out_values[h]], axis=0)
        if slot_rows:
            outgoing, slot_rows[-1], total = lax.optimization_barrier(
                (outgoing, slot_rows[-1], total)
            )
        slot_rows.append(lax.all_gather(outgoing, "seq", axis=1, tiled=True))
    kslot = [g[0].reshape(slots * BLK, head_dim) for g in slot_rows]
    vslot = [jnp.swapaxes(g[1], 0, 1).reshape(head_dim, slots * BLK) for g in slot_rows]
    piece = (proj_rows, width)
    early = kv_local - 1
    step_scratch = pltpu.VMEM((2, rows // HALF, slot_cap * BLK, HALF), jnp.float32)
    if early:
        pairs_seen = early * blocks * rows * slots * BLK
        early_att = pl.pallas_call(
            functools.partial(early_kernel, slot_cap, early),
            out_shape=jax.ShapeDtypeStruct((tok_rows, early * group * head_dim), jnp.bfloat16),
            in_specs=[vmem] * 4 + [smem] + [vmem] * (2 * early),
            out_specs=vmem,
            scratch_shapes=[step_scratch],
            compiler_params=pltpu.CompilerParams(vmem_limit_bytes=32 << 20),
            cost_estimate=pl.CostEstimate(
                flops=8 * pairs_seen * head_dim, transcendentals=pairs_seen, bytes_accessed=10 << 20
            ),
        )(q, top, total, acc, slot_bias, *[x for h in range(early) for x in (kslot[h], vslot[h])])
    else:
        early_att = jnp.zeros((tok_rows, head_dim), jnp.bfloat16)
    return pl.pallas_call(
        functools.partial(attend_kernel, n_head, slot_cap, proj_rows),
        out_shape=jax.ShapeDtypeStruct((tok_rows, width), jnp.bfloat16),
        in_specs=[vmem] * 6 + [smem, vmem] + [pl.BlockSpec(memory_space=pl.ANY)],
        out_specs=vmem,
        scratch_shapes=[
            step_scratch,
            pltpu.VMEM(out_weight.shape, jnp.bfloat16),
            pltpu.VMEM((proj_rows, heads_local * head_dim), jnp.bfloat16),
            pltpu.VMEM((chunks, n_y) + piece, jnp.bfloat16),
            pltpu.VMEM((chunks, n_y) + piece, jnp.bfloat16),
            pltpu.VMEM((chunks, n_y) + piece, jnp.bfloat16),
            pltpu.VMEM((chunks, n_y - 1) + piece, jnp.bfloat16),
            pltpu.VMEM((chunks, n_y - 1) + piece, jnp.bfloat16),
            pltpu.SemaphoreType.DMA,
            pltpu.SemaphoreType.DMA((chunks,)),
            pltpu.SemaphoreType.DMA((chunks,)),
            pltpu.SemaphoreType.DMA((chunks, n_y - 1)),
            pltpu.SemaphoreType.DMA((chunks, n_y - 1)),
        ],
        compiler_params=pltpu.CompilerParams(
            collective_id=0, has_side_effects=True, vmem_limit_bytes=60 << 20
        ),
    )(
        q,
        top,
        total,
        acc,
        kslot[-1],
        vslot[-1],
        slot_bias,
        early_att,
        out_weight,
    )


def solution(mesh):
    return jax.shard_map(
        functools.partial(on_device, mesh.shape["head"]),
        mesh=mesh,
        in_specs=(
            P("seq", "head", None),
            P("seq", "head", None),
            P("seq", "head", None),
            P("head", None),
            P("head", None),
            P("head", None),
        ),
        out_specs=P("seq", "head"),
        check_vma=False,
    )
```
